32 devices in a mesh: ord: 8 (over y, x, core), ch: 4 (over z).
Axes of the slice: x: 2, y: 2, z: 4, core: 2. Of those that a mesh axis runs over, the one named last changes fastest.
Arguments:
- field_grid: bfloat16 [2, 64, 2, 352, 1440], P(None, 'ch', None, 'ord'), may hold values from -40 to 40
- norm_gain: float32 [64], P('ch'), may hold values from 0.1 to 1.9
- norm_bias: float32 [64], P('ch'), may hold values from -3 to 3
- order_table: int32 [512], replicated, may hold values from 0 to 511, as said below
- legendre: bfloat16 [512, 2, 352, 360], P(('ord', 'ch')), may hold values from -0.3125 to 0.3125
Outputs:
- coefficients: bfloat16 [512, 2, 2, 2, 64, 360], P(('ord', 'ch'))
The draws below stay inside these ranges and needn't reach their ends.
Inputs may be any that keep to these rules, and one draw needn't show every extreme that they name: `order_table`: a permutation of the orders in which slots 2 q and 2 q + 1 hold orders p and 511 - p.
All inputs are finite; a program needn't handle non-finite values.
Results may differ from the reference program's by a relative error of at most 0.0062.
Values may be sent and summed in bfloat16 or wider, within the bound.
A program may use at most 128 MiB of HBM per device.

```python
import math
import jax
import jax.numpy as jnp
from jax import lax

B = 2
C = 64
NH = 352
NLON = 1440
M = 512
LH = 360


def draw_field_grid(key, part):
    keys = jax.random.split(key, 3)
    cycles = jnp.arange(NH, dtype=jnp.float32) / NH
    rising = (1.0 + 2.0 * cycles)[None, None, None, :, None]
    drift = (1.0 + cycles)[None, None, None, :, None]
    channel_scale = jnp.exp(jax.random.uniform(keys[1], (1, C, 1, 1, 1), minval=-0.7, maxval=0.7))
    offsets = jax.random.uniform(keys[2], (B, C, 1, 1, 1), minval=0.2, maxval=0.8)
    noise = jax.random.normal(keys[0], (B, C, 2, NH, NLON), jnp.float32)
    values = channel_scale * (rising * noise + offsets * drift)
    return jnp.clip(values, -40.0, 40.0).astype(jnp.bfloat16)


def draw_order_table(key, part):
    paired = jax.random.permutation(key, M // 2).astype(jnp.int32)
    return jnp.stack([paired, M - 1 - paired], axis=1).reshape(M)


def block_levels(key, extent, cuts, low, top_value):
    level = 1.0
    for axis_at, shards_of in cuts:
        steps = jax.random.uniform(jax.random.fold_in(jax.random.fold_in(key, 6), axis_at), (shards_of,), jnp.float32, low / len(cuts), top_value / len(cuts))
        level = level * jnp.repeat(jnp.exp(steps), extent[axis_at] // shards_of).reshape((-1,) + (1,) * (len(extent) - 1 - axis_at))
    return level


def normal_values(stream_key, dims, scale, limit, cuts=(), kind=jnp.bfloat16):
    factor_of = block_levels(stream_key, dims, cuts, -0.22, 0.18) if cuts else 1.0
    entries = jax.random.normal(stream_key, dims, jnp.float32) * scale * factor_of
    return jnp.minimum(jnp.maximum(entries, -limit), limit).astype(kind)


def setup_inputs(seed: int = 0) -> dict:
    seeds = jax.random.split(jax.random.key(seed), 6)
    return {
        "field_grid": draw_field_grid(jax.random.fold_in(seeds[5], 71), 0),
        "norm_gain": jnp.clip(1.0 + 0.18 * jax.random.normal(seeds[1], (C,), jnp.float32), 0.1, 1.9),
        "norm_bias": normal_values(seeds[2], (C,), 0.5, 3.0, ((0, 4),), jnp.float32),
        "order_table": draw_order_table(jax.random.fold_in(seeds[5], 71), 0),
        "legendre": normal_values(seeds[4], (M, 2, NH, LH), NH ** -0.5, 0.3125, ((0, 32),)),
    }


def fourier_table(orders, length):
    sample = jnp.arange(length, dtype=jnp.int32)
    phases = sample[:, None] * orders[None, :].astype(jnp.int32) % length
    angles = phases.astype(jnp.float32) * (2.0 * math.pi / length)
    factor = 1.0 / math.sqrt(length)
    return jnp.concatenate([jnp.cos(angles) * factor, -jnp.sin(angles) * factor], axis=1).astype(jnp.bfloat16)

def legendre_sums(halves_group, legendre_group, orders_group):
    odd_order = orders_group % 2 == 1
    swapped = jnp.where(odd_order[None, None, None, None, None, :], halves_group[:, :, ::-1], halves_group)
    raw_sums = jnp.einsum('bcpirs,spij->sprbcj', swapped.astype(jnp.float32), legendre_group.astype(jnp.float32))
    degree = 2 * jnp.arange(LH, dtype=jnp.int32)[None, :] + jnp.arange(2, dtype=jnp.int32)[:, None]
    allowed = degree[None, :, :] >= orders_group[:, None, None]
    return jnp.where(allowed[:, :, None, None, None, :], raw_sums, 0.0).astype(jnp.bfloat16)

def reference(field_grid, norm_gain, norm_bias, order_table, legendre):
    values = field_grid.astype(jnp.float32)
    average = lax.optimization_barrier(jnp.mean(values, axis=(2, 3, 4), keepdims=True))
    centered = values - average
    spread = lax.optimization_barrier(jnp.mean(centered * centered, axis=(2, 3, 4), keepdims=True))
    normed = (centered * lax.rsqrt(spread + 1e-05) * norm_gain.reshape(1, C, 1, 1, 1) + norm_bias.reshape(1, C, 1, 1, 1)).astype(jnp.bfloat16)
    twiddle = fourier_table(order_table, NLON)
    fourier = jnp.dot(normed.reshape(-1, NLON), twiddle, preferred_element_type=jnp.float32).reshape(B, C, 2, NH, 2, M)
    halves = jnp.stack([fourier[:, :, 0] + fourier[:, :, 1], fourier[:, :, 0] - fourier[:, :, 1]], axis=2).astype(jnp.bfloat16)
    group_width = 16
    group_count = M // group_width
    halves_grouped = jnp.moveaxis(halves.reshape(B, C, 2, NH, 2, group_count, group_width), 5, 0)
    legendre_grouped = legendre.reshape(group_count, group_width, 2, NH, LH)
    orders_grouped = order_table.reshape(group_count, group_width)

    def one_group(pieces):
        return legendre_sums(pieces[0], pieces[1], pieces[2])
    result = lax.map(one_group, (halves_grouped, legendre_grouped, orders_grouped))
    return result.reshape(M, 2, 2, B, C, LH)
```

```python
from functools import partial
import math

import jax
import jax.numpy as jnp
from jax import lax
from jax.experimental import pallas as pl
from jax.experimental.pallas import tpu as pltpu
from jax.sharding import PartitionSpec as P

MESH = pl.DeviceIdType.MESH
LANES = 128
GROUP = 128
QUAD = 4
PITCH = 40


def slot_table(orders, length):
    sample = jnp.arange(length, dtype=jnp.int32)
    phases = sample[:, None] * orders[None, :] % length
    angles = phases.astype(jnp.float32) * (2.0 * math.pi / length)
    factor = 1.0 / math.sqrt(length)
    stacked = jnp.stack([jnp.cos(angles) * factor, -jnp.sin(angles) * factor], axis=2)
    return stacked.reshape(length, 2 * orders.shape[0]).astype(jnp.bfloat16)


def legendre_sums(arrived, legendre, orders):
    odd_order = orders % 2 == 1
    swapped = jnp.where(
        odd_order[:, None, None, None, None, None], arrived[:, :, :, :, ::-1], arrived
    )
    raw_sums = jnp.einsum(
        "srbcpi,spij->sprbcj", swapped, legendre, preferred_element_type=jnp.float32
    )
    half_degrees = legendre.shape[3]
    degree = (
        2 * jnp.arange(half_degrees, dtype=jnp.int32)[None, :]
        + jnp.arange(2, dtype=jnp.int32)[:, None]
    )
    allowed = degree[None, :, :] >= orders[:, None, None]
    return jnp.where(allowed[:, :, None, None, None, :], raw_sums, 0.0).astype(jnp.bfloat16)


def general_path(field_grid, norm_gain, norm_bias, order_table, legendre):
    batch_size, chan_local, hemis, cycle_local, longitudes = field_grid.shape
    order_total = order_table.shape[0]
    values = field_grid.astype(jnp.float32)
    cell_count = hemis * cycle_local * lax.axis_size("ord") * longitudes
    partial_sum = jnp.sum(values, axis=(2, 3, 4))
    totals, squares = lax.psum((partial_sum, jnp.sum(values * values, axis=(2, 3, 4))), "ord")
    average = totals / cell_count
    spread = squares / cell_count - average * average
    centered = values - average[:, :, None, None, None]
    inverse_scale = lax.rsqrt(spread + 1e-05) * norm_gain[None, :]
    normed = (
        centered * inverse_scale[:, :, None, None, None] + norm_bias[None, :, None, None, None]
    ).astype(jnp.bfloat16)
    twiddle = slot_table(order_table, longitudes)
    flat_rows = normed.reshape(-1, longitudes)
    fourier = lax.dot_general(
        twiddle, flat_rows, (((0,), (1,)), ((), ())), preferred_element_type=jnp.float32
    )
    fourier = fourier.reshape(order_total, 2, batch_size, chan_local, hemis, cycle_local)
    north = fourier[:, :, :, :, 0]
    south = fourier[:, :, :, :, 1]
    halves = jnp.stack([north + south, north - south], axis=4).astype(jnp.bfloat16)
    slot_count = legendre.shape[0]
    channel_groups = lax.axis_size("ch")
    first_slot = (lax.axis_index("ord") * channel_groups + lax.axis_index("ch")) * slot_count
    own_orders = lax.dynamic_slice_in_dim(order_table, first_slot, slot_count)
    transform = partial(legendre_sums, legendre=legendre, orders=own_orders)
    arrived = lax.all_to_all(
        lax.all_to_all(halves, "ord", split_axis=0, concat_axis=5, tiled=True),
        "ch",
        split_axis=0,
        concat_axis=3,
        tiled=True,
    )
    return transform(arrived)


def turn(orders, jumps, length):
    product = orders * jumps.astype(jnp.float32)
    left = product - length * jnp.floor(product * (1.0 / length))
    half = (left - length // 2) * (math.pi / length)
    square = half * half
    sine = jnp.full(half.shape, -1.0 / math.factorial(11), jnp.float32)
    for power in (9, 7, 5, 3, 1):
        sine = sine * square + (1.0 if power % 4 == 1 else -1.0) / math.factorial(power)
    sine = sine * half
    cosine = jnp.full(half.shape, 1.0 / math.factorial(12), jnp.float32)
    for power in (10, 8, 6, 4, 2, 0):
        cosine = cosine * square + (1.0 if power % 4 == 0 else -1.0) / math.factorial(power)
    return 2.0 * sine * sine - 1.0, -2.0 * sine * cosine


def exchange_kernel(
    sizes, orders, gains, biases, field, legendre, out,
    grid, rows, packed, twiddle, signs, tsums, columns, sending, arrived, weights, wide, results,
    stats, centers, affine, message, reports, norms, scales, shifts,
    field_sem, report_out_sem, report_in_sem, send_sem, recv_sem, own_sem, weight_sem, out_sem,
):
    n_ord, n_ch, cell_count = sizes
    total = n_ord * n_ch
    fields, cycles, hemis, length = grid.shape
    groups = twiddle.shape[0]
    steps = packed.shape[0]
    slots = legendre.shape[0]
    per_phase = slots // groups
    tiles = rows.shape[0]
    local = gains.shape[0]
    own_ord, own_ch = lax.axis_index("ord"), lax.axis_index("ch")
    me = own_ord * n_ch + own_ch

    chunks = []
    begin = count = 0
    while begin + count < cycles:
        begin += count
        count = min(16 if begin else 8, cycles - begin)
        chunks.append((begin, count))

    def load(part):
        span = pl.ds(*chunks[part])
        return pltpu.make_async_copy(field.at[:, span], grid.at[:, span], field_sem.at[part])

    for part in range(len(chunks)):
        load(part).start()
    weight_load = pltpu.make_async_copy(legendre, weights, weight_sem)

    barrier = pltpu.get_barrier_semaphore()

    def greet(hop, carry):
        peer = lax.rem(me + hop, total)
        pl.semaphore_signal(
            barrier, inc=1, device_id=(peer // n_ch, lax.rem(peer, n_ch)), device_id_type=MESH
        )
        return carry

    lax.fori_loop(1, total, greet, 0)

    lane = lax.broadcasted_iota(jnp.int32, (GROUP, LANES), 1)

    def build(group):
        def put(device, carry):
            for at in range(per_phase):
                slot = device * slots + group * per_phase + at
                row = jnp.full((1, LANES), orders[slot], jnp.int32)
                columns[pl.ds(device * per_phase + at, 1), :] = row
            return carry

        lax.fori_loop(0, total, put, 0)
        order = columns[...].astype(jnp.float32)
        cos_fine, sin_fine = turn(order, lane, length)
        factor = 1.0 / math.sqrt(length)
        cos_fine, sin_fine = cos_fine * factor, sin_fine * factor
        jumps = jnp.where(lane == LANES - 1, length // 2, LANES * jnp.minimum(lane, tiles))
        cos_coarse, sin_coarse = turn(order, jumps, length)
        sign = jnp.where(cos_coarse[:, LANES - 1 :] < 0.0, -1.0, 1.0)
        signs[group] = jnp.broadcast_to(sign, (GROUP, LANES))
        for tile in range(tiles):
            span = slice(tile * LANES, (tile + 1) * LANES)
            cos_at, sin_at = cos_coarse[:, tile : tile + 1], sin_coarse[:, tile : tile + 1]
            twiddle[group, :GROUP, span] = (cos_at * cos_fine - sin_at * sin_fine).astype(jnp.bfloat16)
            twiddle[group, GROUP:, span] = (-(sin_at * cos_fine + cos_at * sin_fine)).astype(jnp.bfloat16)
        cell = lax.broadcasted_iota(jnp.int32, (LANES, tiles * LANES), 1)
        ones = jnp.where(cell < length, 1.0, 0.0).astype(jnp.bfloat16)
        tsums[group] = lax.dot_general(
            twiddle[group], ones, (((1,), (1,)), ((), ())), preferred_element_type=jnp.float32
        )

    for at in range(local):
        affine[at : at + 1, :] = jnp.full((1, LANES), gains[at], jnp.float32)
        affine[local + at : local + at + 1, :] = jnp.full((1, LANES), biases[at], jnp.float32)
    build(0)

    def collect(at, carry, begin, count):
        summed = jnp.zeros((2 * count, LANES), jnp.float32)
        squared = jnp.zeros((2 * count, LANES), jnp.float32)
        for tile in range(tiles):
            piece = grid[at, begin : begin + count, :, tile * LANES : min((tile + 1) * LANES, length)]
            across = piece.shape[2]
            piece = piece.reshape(hemis * count, across).astype(jnp.float32)
            if across < LANES:
                blank = jnp.zeros((hemis * count, LANES - across), jnp.float32)
                piece = jnp.concatenate([piece, blank], axis=1)
            rows[tile, pl.ds(at, hemis * count, stride=PITCH), :] = piece
            summed += piece
            squared += piece * piece
        summed = jnp.sum(summed, axis=0, keepdims=True)
        squared = jnp.sum(squared, axis=0, keepdims=True)
        if begin:
            summed += stats[pl.ds(at, 1), :]
            squared += stats[pl.ds(fields + at, 1), :]
        stats[pl.ds(at, 1), :] = summed
        stats[pl.ds(fields + at, 1), :] = squared
        return carry

    low = lane // fields % 2 == 0
    high = lane // (2 * fields) % 2 == 0

    def swap(mask, upper, lower, amount):
        return (
            jnp.where(mask, upper, pltpu.roll(lower, amount, 1)),
            jnp.where(mask, pltpu.roll(upper, LANES - amount, 1), lower),
        )

    sub = lax.broadcasted_iota(jnp.int32, (GROUP // 8, 8, LANES), 1)
    top = sub < per_phase

    def weave(first, second):
        first, second = first.reshape(GROUP // 8, 8, LANES), second.reshape(GROUP // 8, 8, LANES)
        return (
            jnp.where(top, first, pltpu.roll(second, per_phase, 1)),
            jnp.where(top, pltpu.roll(first, per_phase, 1), second),
        )

    def transform(phase, step, mode):
        spectrum = lax.dot_general(
            twiddle[phase], packed[step], (((1,), (1,)), ((), ())), preferred_element_type=jnp.float32
        )
        sign = signs[phase]
        sign = jnp.concatenate([sign, sign], axis=0)
        north, south = spectrum[:, :LANES], spectrum[:, LANES:] * sign
        scale = norms[mode, 0, :1, :]
        shift = tsums[phase] * norms[mode, 1, :1, :]
        even = (north + south) * scale + jnp.where(sign > 0.0, shift, 0.0)
        odd = (north - south) * scale + jnp.where(sign > 0.0, 0.0, shift)
        a, b, c, d = even[:GROUP], even[GROUP:], odd[:GROUP], odd[GROUP:]
        a, b = swap(low, a, b, fields)
        c, d = swap(low, c, d, fields)
        a, c = swap(high, a, c, 2 * fields)
        b, d = swap(high, b, d, 2 * fields)
        front, back = weave(a, b), weave(c, d)
        for side in range(2):
            both = jnp.concatenate([front[side], back[side]], axis=1)
            sending[phase, :, side, step] = both.astype(jnp.bfloat16)

    lone = n_ch // 2 * n_ord

    def toward(hop):
        ring = lax.rem(own_ch + hop // n_ord + n_ch // 2, n_ch)
        side = lax.rem(own_ord + hop, n_ord)
        return side, ring, side * n_ch + ring

    def send_step(phase, step):
        def send(hop, inner):
            side, ring, peer = toward(hop)
            pltpu.make_async_remote_copy(
                src_ref=sending.at[phase, peer // 2, lax.rem(peer, 2), step],
                dst_ref=arrived.at[phase, own_ch, own_ord, step],
                send_sem=send_sem.at[phase, peer],
                recv_sem=recv_sem.at[phase, me],
                device_id=(side, ring),
                device_id_type=MESH,
            ).start()
            return inner

        lax.fori_loop(0, lone, send, 0)
        lax.fori_loop(lone + 1, total, send, 0)

    def send_phase(phase):
        def send(hop, inner):
            side, ring, peer = toward(hop)
            pltpu.make_async_remote_copy(
                src_ref=sending.at[phase, peer // 2, lax.rem(peer, 2)],
                dst_ref=arrived.at[phase, own_ch, own_ord],
                send_sem=send_sem.at[phase, peer],
                recv_sem=recv_sem.at[phase, me],
                device_id=(side, ring),
                device_id_type=MESH,
            ).start()
            return inner

        lax.fori_loop(0, lone, send, 0)
        lax.fori_loop(lone + 1, total, send, 0)

    def pack(part):
        begin, count = chunks[part]
        load(part).wait()
        lax.fori_loop(0, fields, partial(collect, begin=begin, count=count), 0)

        def place_step(at, carry):
            step = begin // QUAD + at
            for hemi in range(hemis):
                for quarter in range(QUAD):
                    line = (at * QUAD + quarter) * hemis + hemi
                    span = pl.ds(pl.multiple_of(line * PITCH, 8), fields)
                    place = hemi * LANES + quarter * fields
                    for tile in range(tiles):
                        packed[step, place : place + fields, tile * LANES : (tile + 1) * LANES] = rows[
                            tile, span, :
                        ].astype(jnp.bfloat16)
            return carry

        lax.fori_loop(0, count // QUAD, place_step, 0)

    def first_phase(step, carry):
        transform(0, step, 0)
        send_step(0, step)
        return carry

    pack(0)
    sampled = hemis * chunks[0][1] * length
    center = jnp.sum(stats[:fields, :], axis=1, keepdims=True) / sampled
    center = jnp.broadcast_to(center, (fields, LANES))
    centers[...] = center
    across = jnp.concatenate([center] * QUAD, axis=0).T[:8]
    norms[0, 0] = jnp.ones((8, LANES), jnp.float32)
    norms[0, 1] = -2.0 * across

    pl.semaphore_wait(barrier, total - 1)
    early = chunks[0][1] // QUAD
    lax.fori_loop(0, early, first_phase, 0)

    for part in range(1, len(chunks)):
        pack(part)
    weight_load.start()

    local_sums = jnp.broadcast_to(jnp.sum(stats[...], axis=1, keepdims=True), (2 * fields, LANES))
    gathered = jnp.concatenate([local_sums, centers[...], affine[...]], axis=0).T
    message[...] = gathered[:1]
    reports[me] = gathered[:1]

    def report(hop):
        peer = lax.rem(me + hop, total)
        return pltpu.make_async_remote_copy(
            src_ref=message,
            dst_ref=reports.at[me],
            send_sem=report_out_sem.at[peer],
            recv_sem=report_in_sem.at[me],
            device_id=(peer // n_ch, lax.rem(peer, n_ch)),
            device_id_type=MESH,
        )

    def reported(peer):
        return pltpu.make_async_remote_copy(
            src_ref=message,
            dst_ref=reports.at[peer],
            send_sem=report_out_sem.at[peer],
            recv_sem=report_in_sem.at[peer],
            device_id=(peer // n_ch, lax.rem(peer, n_ch)),
            device_id_type=MESH,
        )

    def tell(hop, carry):
        report(hop).start()
        return carry

    lax.fori_loop(1, total, tell, 0)
    lax.fori_loop(early, steps, first_phase, 0)

    spot = lax.broadcasted_iota(jnp.int32, (8, LANES), 1)

    def tile_lanes(values, start, width):
        values = jnp.where((spot >= start) & (spot < start + width), values, 0.0)
        while width < LANES:
            values = values + pltpu.roll(values, width, 1)
            width *= 2
        return values

    def affine_of(source):
        summed = reports[source]
        for at in range(1, n_ord):
            summed = summed + reports[at * n_ch + source]
        summed = jnp.broadcast_to(summed, (8, LANES))
        own = jnp.broadcast_to(reports[source], (8, LANES))
        average = tile_lanes(summed, 0, fields) / cell_count
        spread = tile_lanes(summed, fields, fields) / cell_count - average * average
        gain = tile_lanes(own, 3 * fields, local)
        offset = tile_lanes(own, 3 * fields + local, local)
        return average, lax.rsqrt(spread + 1e-05) * gain, offset

    for hop in range(1, n_ord):
        reported(lax.rem(own_ord + hop, n_ord) * n_ch + own_ch).wait()
    average, scale, offset = affine_of(own_ch)
    norms[1, 0] = scale
    norms[1, 1] = 2.0 * (offset - average * scale)

    def later_phase(phase, carry):
        build(phase)

        def one(step, inner):
            transform(phase, step, 1)
            return inner

        lax.fori_loop(0, steps, one, 0)
        send_phase(phase)
        return carry

    lax.fori_loop(1, groups, later_phase, 0)

    def own_copy(phase):
        return pltpu.make_async_copy(
            sending.at[phase, me // 2, lax.rem(me, 2)], arrived.at[phase, own_ch, own_ord], own_sem.at[phase]
        )

    def out_copy(phase):
        return pltpu.make_async_copy(
            results.at[lax.rem(phase, 2)], out.at[pl.ds(phase * per_phase, per_phase)], out_sem.at[phase]
        )

    for phase in range(groups):
        own_copy(phase).start()
    weight_load.wait()

    def heard(hop, carry):
        others = n_ch - 1
        ring = lax.rem(own_ch + 1 + lax.rem(hop, others), n_ch)
        reported(hop // others * n_ch + ring).wait()
        return carry

    lax.fori_loop(0, n_ord * (n_ch - 1), heard, 0)
    for source in range(n_ch):
        average, scale, offset = affine_of(source)
        scales[source] = scale
        for at in range(n_ord):
            center = tile_lanes(jnp.broadcast_to(reports[at * n_ch + source], (8, LANES)), 2 * fields, fields)
            shift = 2.0 * ((center - average) * scale + offset)
            shifts[source, at * cycles : (at + 1) * cycles, :] = jnp.broadcast_to(shift[:1], (cycles, LANES))

    batch = results.shape[4]
    half = LANES // 2
    depth = n_ord * cycles

    def conclude(phase, carry, raw=False):
        def finish(hop, inner):
            peer = lax.rem(me + hop, total)
            pltpu.make_async_remote_copy(
                src_ref=sending.at[phase, peer // 2, lax.rem(peer, 2)],
                dst_ref=arrived.at[phase, lax.rem(peer, n_ch), peer // n_ch],
                send_sem=send_sem.at[phase, peer],
                recv_sem=recv_sem.at[phase, peer],
                device_id=(peer // n_ch, lax.rem(peer, n_ch)),
                device_id_type=MESH,
            ).wait()
            return inner

        lax.fori_loop(1, total, finish, 0)
        own_copy(phase).wait()

        @pl.when(phase >= 2)
        def _():
            out_copy(phase - 2).wait()

        for source in range(n_ch):
            wide[source] = arrived[phase, source].astype(jnp.float32).reshape(depth * per_phase, LANES)

        def analyze(at, inner):
            slot = phase * per_phase + at
            order = orders[me * slots + slot]
            line = spot[:1]
            if raw:
                row = me * per_phase + at
                real, imag = tsums[0, pl.ds(row, 1), :], tsums[0, pl.ds(GROUP + row, 1), :]
                sign = signs[0, pl.ds(row, 1), :]
                sums = jnp.where(line // fields % 2 == 0, real, imag)
                sums = jnp.where(jnp.where(line < half, sign, -sign) > 0.0, sums, 0.0)

            def turned_rows(source):
                piece = wide[source, pl.ds(at, depth, stride=per_phase), :]
                if raw:
                    piece = piece * scales[source, :1, :] + shifts[source] * sums
                return piece.T.astype(jnp.bfloat16)

            turned = [turned_rows(source) for source in range(n_ch)]
            for parity in range(2):
                left = jnp.concatenate([t[parity * half : (parity + 1) * half] for t in turned], axis=0)
                product = jnp.dot(left, weights[slot, parity], preferred_element_type=jnp.float32)
                degree = 2 * lax.broadcasted_iota(jnp.int32, product.shape, 1) + parity
                product = jnp.where(degree >= order, product, 0.0).astype(jnp.bfloat16)
                for source in range(n_ch):
                    results[lax.rem(phase, 2), at, parity, :, :, source * local : (source + 1) * local, :] = product[
                        source * half : (source + 1) * half
                    ].reshape(2, batch, local, product.shape[1])
            return inner

        lax.fori_loop(0, per_phase, analyze, 0)
        out_copy(phase).start()
        return carry

    conclude(0, 0, raw=True)
    lax.fori_loop(1, groups, conclude, 0)
    for phase in range(groups - 2, groups):
        out_copy(phase).wait()


def emit_kernel(source, target, held, in_sem, out_sem):
    count = held.shape[0]

    def load(at):
        return pltpu.make_async_copy(source.at[at], held.at[at], in_sem.at[at])

    def store(at):
        return pltpu.make_async_copy(held.at[at], target.at[at], out_sem.at[at])

    for at in range(count):
        load(at).start()
    for at in range(count):
        load(at).wait()
        store(at).start()
    for at in range(count):
        store(at).wait()


def kernel_path(field_grid, norm_gain, norm_bias, order_table, legendre):
    batch, local, hemis, cycles, length = field_grid.shape
    n_ord, n_ch = lax.axis_size("ord"), lax.axis_size("ch")
    order_total, slots = order_table.shape[0], legendre.shape[0]
    fields = batch * local
    groups = order_total // GROUP
    tiles = -(-length // LANES)
    steps = cycles // QUAD
    total = n_ord * n_ch
    per_phase = slots // groups
    half_degrees = legendre.shape[3]
    smem = pl.BlockSpec(memory_space=pltpu.SMEM)
    hbm = pl.BlockSpec(memory_space=pltpu.HBM)
    depth = n_ord * cycles
    result = (2, 2, batch, n_ch * local, half_degrees)
    summed = pl.pallas_call(
        partial(exchange_kernel, (n_ord, n_ch, hemis * cycles * n_ord * length)),
        out_shape=jax.ShapeDtypeStruct((slots,) + result, jnp.bfloat16),
        in_specs=[smem, smem, smem, hbm, hbm],
        out_specs=hbm,
        scratch_shapes=[
            pltpu.VMEM((fields, cycles, hemis, length), jnp.bfloat16),
            pltpu.VMEM((tiles, hemis * 16 * PITCH, LANES), jnp.float32),
            pltpu.VMEM((steps, hemis * LANES, tiles * LANES), jnp.bfloat16),
            pltpu.VMEM((groups, 2 * GROUP, tiles * LANES), jnp.bfloat16),
            pltpu.VMEM((groups, GROUP, LANES), jnp.float32),
            pltpu.VMEM((groups, 2 * GROUP, LANES), jnp.float32),
            pltpu.VMEM((GROUP, LANES), jnp.int32),
            pltpu.VMEM((groups, total // 2, 2, steps, QUAD * per_phase, LANES), jnp.bfloat16),
            pltpu.VMEM((groups, n_ch, n_ord, steps, QUAD * per_phase, LANES), jnp.bfloat16),
            pltpu.VMEM(legendre.shape, jnp.bfloat16),
            pltpu.VMEM((n_ch, depth * per_phase, LANES), jnp.float32),
            pltpu.VMEM((2, per_phase) + result, jnp.bfloat16),
            pltpu.VMEM((2 * fields, LANES), jnp.float32),
            pltpu.VMEM((fields, LANES), jnp.float32),
            pltpu.VMEM((2 * local, LANES), jnp.float32),
            pltpu.VMEM((1, LANES), jnp.float32),
            pltpu.VMEM((total, 1, LANES), jnp.float32),
            pltpu.VMEM((2, 2, 8, LANES), jnp.float32),
            pltpu.VMEM((n_ch, 8, LANES), jnp.float32),
            pltpu.VMEM((n_ch, depth, LANES), jnp.float32),
            pltpu.SemaphoreType.DMA((8,)),
            pltpu.SemaphoreType.DMA((total,)),
            pltpu.SemaphoreType.DMA((total,)),
            pltpu.SemaphoreType.DMA((groups, total)),
            pltpu.SemaphoreType.DMA((groups, total)),
            pltpu.SemaphoreType.DMA((groups,)),
            pltpu.SemaphoreType.DMA,
            pltpu.SemaphoreType.DMA((groups,)),
        ],
        compiler_params=pltpu.CompilerParams(
            collective_id=0, has_side_effects=True, vmem_limit_bytes=63 * 2**20
        ),
        name="spectral_analysis",
    )(order_table, norm_gain, norm_bias, field_grid.transpose(0, 1, 3, 2, 4).reshape(fields, cycles, hemis, length), legendre)
    return pl.pallas_call(
        emit_kernel,
        out_shape=jax.ShapeDtypeStruct(summed.shape, summed.dtype),
        in_specs=[hbm],
        out_specs=hbm,
        scratch_shapes=[
            pltpu.VMEM(summed.shape, summed.dtype),
            pltpu.SemaphoreType.DMA((slots,)),
            pltpu.SemaphoreType.DMA((slots,)),
        ],
        name="emit_result",
    )(summed)


def on_device(field_grid, norm_gain, norm_bias, order_table, legendre):
    batch, local, hemis, cycles, _ = field_grid.shape
    fits = (
        batch == 2
        and batch * local * QUAD == LANES
        and hemis == 2
        and cycles % QUAD == 0
        and legendre.shape[0] == 16
        and order_table.shape[0] == 4 * GROUP
        and field_grid.shape[4] <= LANES * (LANES - 1)
        and field_grid.shape[4] % 2 == 0
    )
    path = kernel_path if fits else general_path
    return path(field_grid, norm_gain, norm_bias, order_table, legendre)


def solution(mesh):
    placed = (
        P(None, "ch", None, "ord", None),
        P("ch"),
        P("ch"),
        P(),
        P(("ord", "ch"), None, None, None),
    )
    return jax.shard_map(
        on_device,
        mesh=mesh,
        in_specs=placed,
        out_specs=P(("ord", "ch"), None, None, None, None, None),
        check_vma=False,
    )
```

```python
from functools import partial
import math

import jax
import jax.numpy as jnp
from jax import lax
from jax.experimental import pallas as pl
from jax.experimental.pallas import tpu as pltpu
from jax.sharding import PartitionSpec as P

MESH = pl.DeviceIdType.MESH
LANES = 128
GROUP = 128
QUAD = 4
PITCH = 40
RAW = 2


def slot_table(orders, length):
    sample = jnp.arange(length, dtype=jnp.int32)
    phases = sample[:, None] * orders[None, :] % length
    angles = phases.astype(jnp.float32) * (2.0 * math.pi / length)
    factor = 1.0 / math.sqrt(length)
    stacked = jnp.stack([jnp.cos(angles) * factor, -jnp.sin(angles) * factor], axis=2)
    return stacked.reshape(length, 2 * orders.shape[0]).astype(jnp.bfloat16)


def legendre_sums(arrived, legendre, orders):
    odd_order = orders % 2 == 1
    swapped = jnp.where(
        odd_order[:, None, None, None, None, None], arrived[:, :, :, :, ::-1], arrived
    )
    raw_sums = jnp.einsum(
        "srbcpi,spij->sprbcj", swapped, legendre, preferred_element_type=jnp.float32
    )
    half_degrees = legendre.shape[3]
    degree = (
        2 * jnp.arange(half_degrees, dtype=jnp.int32)[None, :]
        + jnp.arange(2, dtype=jnp.int32)[:, None]
    )
    allowed = degree[None, :, :] >= orders[:, None, None]
    return jnp.where(allowed[:, :, None, None, None, :], raw_sums, 0.0).astype(jnp.bfloat16)


def general_path(field_grid, norm_gain, norm_bias, order_table, legendre):
    batch_size, chan_local, hemis, cycle_local, longitudes = field_grid.shape
    order_total = order_table.shape[0]
    values = field_grid.astype(jnp.float32)
    cell_count = hemis * cycle_local * lax.axis_size("ord") * longitudes
    partial_sum = jnp.sum(values, axis=(2, 3, 4))
    totals, squares = lax.psum((partial_sum, jnp.sum(values * values, axis=(2, 3, 4))), "ord")
    average = totals / cell_count
    spread = squares / cell_count - average * average
    centered = values - average[:, :, None, None, None]
    inverse_scale = lax.rsqrt(spread + 1e-05) * norm_gain[None, :]
    normed = (
        centered * inverse_scale[:, :, None, None, None] + norm_bias[None, :, None, None, None]
    ).astype(jnp.bfloat16)
    twiddle = slot_table(order_table, longitudes)
    flat_rows = normed.reshape(-1, longitudes)
    fourier = lax.dot_general(
        twiddle, flat_rows, (((0,), (1,)), ((), ())), preferred_element_type=jnp.float32
    )
    fourier = fourier.reshape(order_total, 2, batch_size, chan_local, hemis, cycle_local)
    north = fourier[:, :, :, :, 0]
    south = fourier[:, :, :, :, 1]
    halves = jnp.stack([north + south, north - south], axis=4).astype(jnp.bfloat16)
    slot_count = legendre.shape[0]
    channel_groups = lax.axis_size("ch")
    first_slot = (lax.axis_index("ord") * channel_groups + lax.axis_index("ch")) * slot_count
    own_orders = lax.dynamic_slice_in_dim(order_table, first_slot, slot_count)
    transform = partial(legendre_sums, legendre=legendre, orders=own_orders)
    arrived = lax.all_to_all(
        lax.all_to_all(halves, "ord", split_axis=0, concat_axis=5, tiled=True),
        "ch",
        split_axis=0,
        concat_axis=3,
        tiled=True,
    )
    return transform(arrived)


def turn(orders, jumps, length):
    product = orders * jumps.astype(jnp.float32)
    left = product - length * jnp.floor(product * (1.0 / length))
    half = (left - length // 2) * (math.pi / length)
    square = half * half
    sine = jnp.full(half.shape, -1.0 / math.factorial(11), jnp.float32)
    for power in (9, 7, 5, 3, 1):
        sine = sine * square + (1.0 if power % 4 == 1 else -1.0) / math.factorial(power)
    sine = sine * half
    cosine = jnp.full(half.shape, 1.0 / math.factorial(12), jnp.float32)
    for power in (10, 8, 6, 4, 2, 0):
        cosine = cosine * square + (1.0 if power % 4 == 0 else -1.0) / math.factorial(power)
    return 2.0 * sine * sine - 1.0, -2.0 * sine * cosine


def exchange_kernel(
    sizes, orders, gains, biases, field, legendre, out,
    grid, rows, packed, twiddle, signs, tsums, columns, sending, arrived, weights, wide, left,
    stats, centers, affine, message, reports, norms, scales, shifts,
    field_sem, report_out_sem, report_in_sem, send_sem, recv_sem, own_sem, weight_sem,
):
    n_ord, n_ch, cell_count = sizes
    total = n_ord * n_ch
    fields, cycles, hemis, length = grid.shape
    groups = twiddle.shape[0]
    steps = packed.shape[0]
    slots = legendre.shape[0]
    per_phase = slots // groups
    tiles = rows.shape[0]
    local = gains.shape[0]
    own_ord, own_ch = lax.axis_index("ord"), lax.axis_index("ch")
    me = own_ord * n_ch + own_ch

    chunks = []
    begin = count = 0
    while begin + count < cycles:
        begin += count
        count = min(max(len(chunks), 1) * QUAD, 4 * QUAD, cycles - begin)
        chunks.append((begin, count))

    def load(part):
        span = pl.ds(*chunks[part])
        return pltpu.make_async_copy(field.at[:, span], grid.at[:, span], field_sem.at[part])

    for part in range(len(chunks)):
        load(part).start()
    weight_load = pltpu.make_async_copy(legendre, weights, weight_sem)

    barrier = pltpu.get_barrier_semaphore()

    def greet(hop, carry):
        peer = lax.rem(me + hop, total)
        pl.semaphore_signal(
            barrier, inc=1, device_id=(peer // n_ch, lax.rem(peer, n_ch)), device_id_type=MESH
        )
        return carry

    lax.fori_loop(1, total, greet, 0)

    lane = lax.broadcasted_iota(jnp.int32, (GROUP, LANES), 1)

    def build(group):
        def put(device, carry):
            for at in range(per_phase):
                slot = device * slots + group * per_phase + at
                row = jnp.full((1, LANES), orders[slot], jnp.int32)
                columns[pl.ds(device * per_phase + at, 1), :] = row
            return carry

        lax.fori_loop(0, total, put, 0)
        order = columns[...].astype(jnp.float32)
        cos_fine, sin_fine = turn(order, lane, length)
        factor = 1.0 / math.sqrt(length)
        cos_fine, sin_fine = cos_fine * factor, sin_fine * factor
        jumps = jnp.where(lane == LANES - 1, length // 2, LANES * jnp.minimum(lane, tiles))
        cos_coarse, sin_coarse = turn(order, jumps, length)
        sign = jnp.where(cos_coarse[:, LANES - 1 :] < 0.0, -1.0, 1.0)
        signs[group] = jnp.broadcast_to(sign, (GROUP, LANES))
        for tile in range(tiles):
            span = slice(tile * LANES, (tile + 1) * LANES)
            cos_at, sin_at = cos_coarse[:, tile : tile + 1], sin_coarse[:, tile : tile + 1]
            twiddle[group, :GROUP, span] = (cos_at * cos_fine - sin_at * sin_fine).astype(jnp.bfloat16)
            twiddle[group, GROUP:, span] = (-(sin_at * cos_fine + cos_at * sin_fine)).astype(jnp.bfloat16)
        cell = lax.broadcasted_iota(jnp.int32, (LANES, tiles * LANES), 1)
        ones = jnp.where(cell < length, 1.0, 0.0).astype(jnp.bfloat16)
        tsums[group] = lax.dot_general(
            twiddle[group], ones, (((1,), (1,)), ((), ())), preferred_element_type=jnp.float32
        )

    for at in range(local):
        affine[at : at + 1, :] = jnp.full((1, LANES), gains[at], jnp.float32)
        affine[local + at : local + at + 1, :] = jnp.full((1, LANES), biases[at], jnp.float32)
    build(0)

    def collect(at, carry, begin, count):
        summed = jnp.zeros((2 * count, LANES), jnp.float32)
        squared = jnp.zeros((2 * count, LANES), jnp.float32)
        for tile in range(tiles):
            piece = grid[at, begin : begin + count, :, tile * LANES : min((tile + 1) * LANES, length)]
            across = piece.shape[2]
            piece = piece.reshape(hemis * count, across).astype(jnp.float32)
            if across < LANES:
                blank = jnp.zeros((hemis * count, LANES - across), jnp.float32)
                piece = jnp.concatenate([piece, blank], axis=1)
            rows[tile, pl.ds(at, hemis * count, stride=PITCH), :] = piece
            summed += piece
            squared += piece * piece
        summed = jnp.sum(summed, axis=0, keepdims=True)
        squared = jnp.sum(squared, axis=0, keepdims=True)
        if begin:
            summed += stats[pl.ds(at, 1), :]
            squared += stats[pl.ds(fields + at, 1), :]
        stats[pl.ds(at, 1), :] = summed
        stats[pl.ds(fields + at, 1), :] = squared
        return carry

    low = lane // fields % 2 == 0
    high = lane // (2 * fields) % 2 == 0

    def swap(mask, upper, lower, amount):
        return (
            jnp.where(mask, upper, pltpu.roll(lower, amount, 1)),
            jnp.where(mask, pltpu.roll(upper, LANES - amount, 1), lower),
        )

    sub = lax.broadcasted_iota(jnp.int32, (GROUP // 8, 8, LANES), 1)
    top = sub < per_phase

    def weave(first, second):
        first, second = first.reshape(GROUP // 8, 8, LANES), second.reshape(GROUP // 8, 8, LANES)
        return (
            jnp.where(top, first, pltpu.roll(second, per_phase, 1)),
            jnp.where(top, pltpu.roll(first, per_phase, 1), second),
        )

    def transform(phase, step, mode):
        spectrum = lax.dot_general(
            twiddle[phase], packed[step], (((1,), (1,)), ((), ())), preferred_element_type=jnp.float32
        )
        sign = signs[phase]
        sign = jnp.concatenate([sign, sign], axis=0)
        north, south = spectrum[:, :LANES], spectrum[:, LANES:] * sign
        scale = norms[mode, 0, :1, :]
        shift = tsums[phase] * norms[mode, 1, :1, :]
        even = (north + south) * scale + jnp.where(sign > 0.0, shift, 0.0)
        odd = (north - south) * scale + jnp.where(sign > 0.0, 0.0, shift)
        a, b, c, d = even[:GROUP], even[GROUP:], odd[:GROUP], odd[GROUP:]
        a, b = swap(low, a, b, fields)
        c, d = swap(low, c, d, fields)
        a, c = swap(high, a, c, 2 * fields)
        b, d = swap(high, b, d, 2 * fields)
        front, back = weave(a, b), weave(c, d)
        for side in range(2):
            both = jnp.concatenate([front[side], back[side]], axis=1)
            sending[phase, :, side, step] = both.astype(jnp.bfloat16)

    lone = n_ch // 2 * n_ord

    def partner(turned):
        low_bit = lax.rem(own_ch + turned, 2)
        high_bit = lax.rem(own_ch // 2 + turned // 2, 2)
        return 2 * high_bit + low_bit

    def toward(hop):
        ring = partner(lax.rem(hop // n_ord + n_ch // 2, n_ch))
        side = lax.rem(own_ord + hop, n_ord)
        return side, ring, side * n_ch + ring

    def send_part(part):
        span = pl.ds(chunks[part][0] // QUAD, chunks[part][1] // QUAD)

        def send(hop, inner):
            side, ring, peer = toward(hop)
            pltpu.make_async_remote_copy(
                src_ref=sending.at[0, peer // 2, lax.rem(peer, 2), span],
                dst_ref=arrived.at[0, own_ch, own_ord, span],
                send_sem=send_sem.at[0, peer],
                recv_sem=recv_sem.at[0, me],
                device_id=(side, ring),
                device_id_type=MESH,
            ).start()
            return inner

        lax.fori_loop(0, lone, send, 0)
        lax.fori_loop(lone + 1, total, send, 0)

    def send_phase(phase):
        def send(hop, inner):
            side, ring, peer = toward(hop)
            pltpu.make_async_remote_copy(
                src_ref=sending.at[phase, peer // 2, lax.rem(peer, 2)],
                dst_ref=arrived.at[phase, own_ch, own_ord],
                send_sem=send_sem.at[phase, peer],
                recv_sem=recv_sem.at[phase, me],
                device_id=(side, ring),
                device_id_type=MESH,
            ).start()
            return inner

        lax.fori_loop(0, lone, send, 0)
        lax.fori_loop(lone + 1, total, send, 0)

    def pack(part):
        begin, count = chunks[part]
        load(part).wait()
        lax.fori_loop(0, fields, partial(collect, begin=begin, count=count), 0)

        def place_step(at, carry):
            step = begin // QUAD + at
            for hemi in range(hemis):
                for quarter in range(QUAD):
                    line = (at * QUAD + quarter) * hemis + hemi
                    span = pl.ds(pl.multiple_of(line * PITCH, 8), fields)
                    place = hemi * LANES + quarter * fields
                    for tile in range(tiles):
                        packed[step, place : place + fields, tile * LANES : (tile + 1) * LANES] = rows[
                            tile, span, :
                        ].astype(jnp.bfloat16)
            return carry

        lax.fori_loop(0, count // QUAD, place_step, 0)

    def first_phase(step, carry):
        transform(0, step, 0)
        return carry

    pack(0)
    sampled = hemis * chunks[0][1] * length
    center = jnp.sum(stats[:fields, :], axis=1, keepdims=True) / sampled
    center = jnp.broadcast_to(center, (fields, LANES))
    centers[...] = center
    across = jnp.concatenate([center] * QUAD, axis=0).T[:8]
    norms[0, 0] = jnp.ones((8, LANES), jnp.float32)
    norms[0, 1] = -2.0 * across

    pl.semaphore_wait(barrier, total - 1)
    lax.fori_loop(0, chunks[0][1] // QUAD, first_phase, 0)
    send_part(0)
    for part in range(1, len(chunks)):
        pack(part)
        begin, count = chunks[part]
        lax.fori_loop(begin // QUAD, (begin + count) // QUAD, first_phase, 0)
        send_part(part)
    weight_load.start()

    local_sums = jnp.broadcast_to(jnp.sum(stats[...], axis=1, keepdims=True), (2 * fields, LANES))
    gathered = jnp.concatenate([local_sums, centers[...], affine[...]], axis=0).T
    message[...] = gathered[:1]
    reports[me] = gathered[:1]

    def report(hop):
        peer = lax.rem(me + hop, total)
        return pltpu.make_async_remote_copy(
            src_ref=message,
            dst_ref=reports.at[me],
            send_sem=report_out_sem.at[peer],
            recv_sem=report_in_sem.at[me],
            device_id=(peer // n_ch, lax.rem(peer, n_ch)),
            device_id_type=MESH,
        )

    def reported(peer):
        return pltpu.make_async_remote_copy(
            src_ref=message,
            dst_ref=reports.at[peer],
            send_sem=report_out_sem.at[peer],
            recv_sem=report_in_sem.at[peer],
            device_id=(peer // n_ch, lax.rem(peer, n_ch)),
            device_id_type=MESH,
        )

    def tell(hop, carry):
        report(hop).start()
        return carry

    lax.fori_loop(1, total, tell, 0)

    spot = lax.broadcasted_iota(jnp.int32, (8, LANES), 1)

    def tile_lanes(values, start, width):
        values = jnp.where((spot >= start) & (spot < start + width), values, 0.0)
        while width < LANES:
            values = values + pltpu.roll(values, width, 1)
            width *= 2
        return values

    def affine_of(source):
        summed = reports[source]
        for at in range(1, n_ord):
            summed = summed + reports[at * n_ch + source]
        summed = jnp.broadcast_to(summed, (8, LANES))
        own = jnp.broadcast_to(reports[source], (8, LANES))
        average = tile_lanes(summed, 0, fields) / cell_count
        spread = tile_lanes(summed, fields, fields) / cell_count - average * average
        gain = tile_lanes(own, 3 * fields, local)
        offset = tile_lanes(own, 3 * fields + local, local)
        return average, lax.rsqrt(spread + 1e-05) * gain, offset

    def later_phase(phase, carry, mode):
        build(phase)

        def one(step, inner):
            transform(phase, step, mode)
            return inner

        lax.fori_loop(0, steps, one, 0)
        send_phase(phase)
        return carry

    lax.fori_loop(1, RAW, partial(later_phase, mode=0), 0)
    for hop in range(1, n_ord):
        reported(lax.rem(own_ord + hop, n_ord) * n_ch + own_ch).wait()
    average, scale, offset = affine_of(own_ch)
    norms[1, 0] = scale
    norms[1, 1] = 2.0 * (offset - average * scale)
    lax.fori_loop(RAW, groups, partial(later_phase, mode=1), 0)

    def own_copy(phase):
        return pltpu.make_async_copy(
            sending.at[phase, me // 2, lax.rem(me, 2)], arrived.at[phase, own_ch, own_ord], own_sem.at[phase]
        )

    for phase in range(groups):
        own_copy(phase).start()
    weight_load.wait()

    def heard(hop, carry):
        others = n_ch - 1
        ring = lax.rem(own_ch + 1 + lax.rem(hop, others), n_ch)
        reported(hop // others * n_ch + ring).wait()
        return carry

    lax.fori_loop(0, n_ord * (n_ch - 1), heard, 0)
    for source in range(n_ch):
        average, scale, offset = affine_of(source)
        scales[source] = scale
        for at in range(n_ord):
            center = tile_lanes(jnp.broadcast_to(reports[at * n_ch + source], (8, LANES)), 2 * fields, fields)
            shift = 2.0 * ((center - average) * scale + offset)
            shifts[source, at * cycles : (at + 1) * cycles, :] = jnp.broadcast_to(shift[:1], (cycles, LANES))

    batch = out.shape[3]
    half = LANES // 2
    depth = n_ord * cycles

    def conclude(phase, carry, raw=False):
        own_copy(phase).wait()

        line = spot[:1]
        for turned in range(n_ch):
            source = partner(turned)

            def receive(at, inner, source=source, turned=turned):
                peer = lax.rem(own_ord + at, n_ord) * n_ch + source
                pltpu.make_async_remote_copy(
                    src_ref=sending.at[phase, peer // 2, lax.rem(peer, 2)],
                    dst_ref=arrived.at[phase, source, peer // n_ch],
                    send_sem=send_sem.at[phase, peer],
                    recv_sem=recv_sem.at[phase, peer],
                    device_id=(peer // n_ch, source),
                    device_id_type=MESH,
                ).wait_recv()
                return inner

            lax.fori_loop(0 if turned else 1, n_ord, receive, 0)
            wide[turned % 2] = arrived[phase, source].astype(jnp.float32).reshape(depth * per_phase, LANES)
            for at in range(per_phase):
                piece = wide[turned % 2, pl.ds(at, depth, stride=per_phase), :]
                if raw:
                    row = me * per_phase + at
                    real, imag = tsums[phase, pl.ds(row, 1), :], tsums[phase, pl.ds(GROUP + row, 1), :]
                    sign = signs[phase, pl.ds(row, 1), :]
                    sums = jnp.where(line // fields % 2 == 0, real, imag)
                    sums = jnp.where(jnp.where(line < half, sign, -sign) > 0.0, sums, 0.0)
                    piece = piece * scales[source, :1, :] + shifts[source] * sums
                piece = piece.T.astype(jnp.bfloat16)
                span = pl.ds(pl.multiple_of(source * half, half), half)
                for parity in range(2):
                    left[at, parity, span, :] = piece[parity * half : (parity + 1) * half]

        def analyze(at, inner):
            slot = phase * per_phase + at
            order = orders[me * slots + slot]
            for parity in range(2):
                product = jnp.dot(left[at, parity], weights[slot, parity], preferred_element_type=jnp.float32)
                degree = 2 * lax.broadcasted_iota(jnp.int32, product.shape, 1) + parity
                product = jnp.where(degree >= order, product, 0.0).astype(jnp.bfloat16)
                for source in range(n_ch):
                    out[slot, parity, :, :, source * local : (source + 1) * local, :] = product[
                        source * half : (source + 1) * half
                    ].reshape(2, batch, local, product.shape[1])
            return inner

        lax.fori_loop(0, per_phase, analyze, 0)
        return carry

    lax.fori_loop(0, RAW, partial(conclude, raw=True), 0)
    lax.fori_loop(RAW, groups, conclude, 0)

    def drain(at, carry):
        phase, hop = at // (total - 1), 1 + lax.rem(at, total - 1)
        peer = lax.rem(me + hop, total)
        pltpu.make_async_remote_copy(
            src_ref=sending.at[phase, peer // 2, lax.rem(peer, 2)],
            dst_ref=arrived.at[phase, own_ch, own_ord],
            send_sem=send_sem.at[phase, peer],
            recv_sem=recv_sem.at[phase, peer],
            device_id=(peer // n_ch, lax.rem(peer, n_ch)),
            device_id_type=MESH,
        ).wait_send()
        return carry

    lax.fori_loop(0, groups * (total - 1), drain, 0)


def kernel_path(field_grid, norm_gain, norm_bias, order_table, legendre):
    batch, local, hemis, cycles, length = field_grid.shape
    n_ord, n_ch = lax.axis_size("ord"), lax.axis_size("ch")
    order_total, slots = order_table.shape[0], legendre.shape[0]
    fields = batch * local
    groups = order_total // GROUP
    tiles = -(-length // LANES)
    steps = cycles // QUAD
    total = n_ord * n_ch
    per_phase = slots // groups
    half_degrees = legendre.shape[3]
    smem = pl.BlockSpec(memory_space=pltpu.SMEM)
    hbm = pl.BlockSpec(memory_space=pltpu.HBM)
    vmem = pl.BlockSpec(memory_space=pltpu.VMEM)
    depth = n_ord * cycles
    result = (2, 2, batch, n_ch * local, half_degrees)
    summed = pl.pallas_call(
        partial(exchange_kernel, (n_ord, n_ch, hemis * cycles * n_ord * length)),
        out_shape=pltpu.VMEM((slots,) + result, jnp.bfloat16),
        in_specs=[smem, smem, smem, hbm, hbm],
        out_specs=vmem,
        scratch_shapes=[
            pltpu.VMEM((fields, cycles, hemis, length), jnp.bfloat16),
            pltpu.VMEM((tiles, hemis * 16 * PITCH, LANES), jnp.float32),
            pltpu.VMEM((steps, hemis * LANES, tiles * LANES), jnp.bfloat16),
            pltpu.VMEM((groups, 2 * GROUP, tiles * LANES), jnp.bfloat16),
            pltpu.VMEM((groups, GROUP, LANES), jnp.float32),
            pltpu.VMEM((groups, 2 * GROUP, LANES), jnp.float32),
            pltpu.VMEM((GROUP, LANES), jnp.int32),
            pltpu.VMEM((groups, total // 2, 2, steps, QUAD * per_phase, LANES), jnp.bfloat16),
            pltpu.VMEM((groups, n_ch, n_ord, steps, QUAD * per_phase, LANES), jnp.bfloat16),
            pltpu.VMEM(legendre.shape, jnp.bfloat16),
            pltpu.VMEM((2, depth * per_phase, LANES), jnp.float32),
            pltpu.VMEM((per_phase, 2, n_ch * LANES // 2, depth), jnp.bfloat16),
            pltpu.VMEM((2 * fields, LANES), jnp.float32),
            pltpu.VMEM((fields, LANES), jnp.float32),
            pltpu.VMEM((2 * local, LANES), jnp.float32),
            pltpu.VMEM((1, LANES), jnp.float32),
            pltpu.VMEM((total, 1, LANES), jnp.float32),
            pltpu.VMEM((2, 2, 8, LANES), jnp.float32),
            pltpu.VMEM((n_ch, 8, LANES), jnp.float32),
            pltpu.VMEM((n_ch, depth, LANES), jnp.float32),
            pltpu.SemaphoreType.DMA((8,)),
            pltpu.SemaphoreType.DMA((total,)),
            pltpu.SemaphoreType.DMA((total,)),
            pltpu.SemaphoreType.DMA((groups, total)),
            pltpu.SemaphoreType.DMA((groups, total)),
            pltpu.SemaphoreType.DMA((groups,)),
            pltpu.SemaphoreType.DMA,
        ],
        compiler_params=pltpu.CompilerParams(
            collective_id=0, has_side_effects=True, vmem_limit_bytes=56 * 2**20
        ),
        name="spectral_analysis",
    )(order_table, norm_gain, norm_bias, field_grid.transpose(0, 1, 3, 2, 4).reshape(fields, cycles, hemis, length), legendre)
    return summed


def on_device(field_grid, norm_gain, norm_bias, order_table, legendre):
    batch, local, hemis, cycles, _ = field_grid.shape
    fits = (
        batch == 2
        and lax.axis_size("ch") == 4
        and batch * local * QUAD == LANES
        and hemis == 2
        and cycles % QUAD == 0
        and legendre.shape[0] == 16
        and order_table.shape[0] == 4 * GROUP
        and field_grid.shape[4] <= LANES * (LANES - 1)
        and field_grid.shape[4] % 2 == 0
    )
    path = kernel_path if fits else general_path
    return path(field_grid, norm_gain, norm_bias, order_table, legendre)


def solution(mesh):
    placed = (
        P(None, "ch", None, "ord", None),
        P("ch"),
        P("ch"),
        P(),
        P(("ord", "ch"), None, None, None),
    )
    return jax.shard_map(
        on_device,
        mesh=mesh,
        in_specs=placed,
        out_specs=P(("ord", "ch"), None, None, None, None, None),
        check_vma=False,
    )
```
